512 devices in a mesh: dp: 8 (over z), expert: 64 (over y, x, core).
Axes of the slice: x: 4, y: 8, z: 8, core: 2. Of those that a mesh axis runs over, the one named last changes fastest.
Arguments:
- tokens: bfloat16 [65536, 3584], P(('dp', 'expert')), may hold values from -6 to 6
- cotangent: bfloat16 [65536, 3584], P(('dp', 'expert')), may hold values from -6 to 6
- route_ids: int32 [65536, 8], P(('dp', 'expert')), may hold values from 0 to 255, as said below
- route_gates: float32 [65536, 8], P(('dp', 'expert')), may hold values from 0.1 to 1
- gate_w: bfloat16 [3584, 8192], P('dp', 'expert'), may hold values from -0.09375 to 0.09375
- up_w: bfloat16 [3584, 8192], P('dp', 'expert'), may hold values from -0.09375 to 0.09375
- down_w: bfloat16 [3584, 8192], P('dp', 'expert'), may hold values from -0.1875 to 0.1875
Outputs:
- moe_out: bfloat16 [65536, 3584], P(('dp', 'expert'))
- d_tokens: bfloat16 [65536, 3584], P(('dp', 'expert'))
- d_gates: float32 [65536, 8], P(('dp', 'expert'))
- d_gate_w: bfloat16 [3584, 8192], P('dp', 'expert')
- d_up_w: bfloat16 [3584, 8192], P('dp', 'expert')
- d_down_w: bfloat16 [3584, 8192], P('dp', 'expert')
The draws below stay inside these ranges and needn't reach their ends.
Inputs may be any that keep to these rules, and one draw needn't show every extreme that they name: `route_ids`: each token names 8 different experts; the experts in flight are 0 to 7. Among the tokens of one device (aligned blocks of 128 tokens) each expert in flight is named by at most 6 tokens, and in every draw one expert in flight is named by exactly 6 tokens in every block.
All inputs are finite; a program needn't handle non-finite values.
Results may differ from the reference program's by a relative error of at most 0.017.
Values may be sent and summed in bfloat16 or wider, within the bound.
A program may use at most 64 MiB of HBM per device.

```python
import math
import jax
import jax.numpy as jnp
from jax import lax

D = 3584
H = 1024
ROUTED = 256
TOP = 8
SLICES = 8
TOK_DEV = 128
HID_DEV = 128
EXPERTS = 8
CAP = 6
TOKENS = 65536
N_DP = 8
N_EXPERT = 64


def draw_route_ids(key, part):
    blocks = TOKENS // TOK_DEV
    per_dp = blocks // N_DP
    key_list = jax.random.split(key, 6)
    full_expert = jax.random.randint(key_list[0], (N_DP,), 0, EXPERTS)
    block_full = full_expert[jnp.arange(blocks) // per_dp]
    expert_loads = jax.random.randint(key_list[1], (blocks, EXPERTS), CAP // 2, CAP + 1)
    full_offset = jax.random.randint(key_list[5], (), 0, 4)
    full_block = jnp.arange(blocks) % 4 == full_offset
    at_most = (jnp.arange(EXPERTS)[None, :] == block_full[:, None]) | full_block[:, None]
    expert_loads = jnp.where(at_most, CAP, expert_loads)
    order_keys = jax.random.randint(key_list[2], (blocks, TOK_DEV, EXPERTS), 0, 2 ** 20) * TOK_DEV + jnp.arange(TOK_DEV)[None, :, None]
    rank_in_block = jnp.argsort(jnp.argsort(order_keys, axis=1), axis=1)
    member = (rank_in_block < expert_loads[:, None, :]).astype(jnp.int32).reshape(TOKENS, EXPERTS)
    window_count = jnp.sum(member, axis=1)
    position = jnp.cumsum(member, axis=1) - 1
    picked = ((member[:, None, :] == 1) & (position[:, None, :] == jnp.arange(TOP)[None, :, None])).astype(jnp.int32)
    window_ids = jnp.sum(picked * jnp.arange(EXPERTS)[None, None, :], axis=2)
    outside = ROUTED - EXPERTS
    scores = jax.random.randint(key_list[3], (TOKENS, outside), 0, 2 ** 20) * outside + jnp.arange(outside)[None, :]
    chosen = EXPERTS + lax.top_k(scores, TOP)[1]
    slot_index = jnp.arange(TOP)[None, :]
    filler = jnp.take_along_axis(chosen, jnp.clip(slot_index - window_count[:, None], 0, TOP - 1), axis=1)
    ordered = jnp.where(slot_index < window_count[:, None], window_ids, filler)
    shuffle_keys = jax.random.randint(key_list[4], (TOKENS, TOP), 0, 2 ** 20) * TOP + slot_index
    shuffle_order = jnp.argsort(shuffle_keys, axis=1)
    return jnp.take_along_axis(ordered, shuffle_order, axis=1).astype(jnp.int32)


def block_scale(own_key, dims, pieces, low, largest):
    factor_of = 1.0
    for dim, parts in pieces:
        steps = jax.random.uniform(jax.random.fold_in(jax.random.fold_in(own_key, 6), dim), (parts,), jnp.float32, low / len(pieces), largest / len(pieces))
        factor_of = factor_of * jnp.repeat(jnp.exp(steps), dims[dim] // parts).reshape((-1,) + (1,) * (len(dims) - 1 - dim))
    return factor_of


def scatter_about(own_key, shape, scale, reach, shards=(), held_as=jnp.bfloat16):
    result = scale * jax.random.normal(own_key, shape, jnp.float32)
    if shards:
        result = result * block_scale(own_key, shape, shards, -0.22, 0.18)
    return jnp.clip(result, -reach, reach).astype(held_as)


def setup_inputs(seed: int = 0) -> dict:
    key_of = jax.random.split(jax.random.key(seed), 8)
    return {
        "tokens": scatter_about(key_of[0], (TOKENS, D), 1.0, 6.0, ((0, 512),)),
        "cotangent": scatter_about(key_of[1], (TOKENS, D), 1.0, 6.0, ((0, 512),)),
        "route_ids": draw_route_ids(jax.random.fold_in(key_of[7], 71), 0),
        "route_gates": jnp.clip(jnp.exp(math.log(1.0) - 2.3025851 * jax.random.uniform(key_of[3], (TOKENS, TOP), jnp.float32) ** block_scale(key_of[3], (TOKENS, TOP), ((0, 512),), -0.2, 0.2)), 0.1, 1.0),
        "gate_w": scatter_about(key_of[4], (D, EXPERTS * H), D ** -0.5, 0.09375, ((0, 8), (1, 64))),
        "up_w": scatter_about(key_of[5], (D, EXPERTS * H), D ** -0.5, 0.09375, ((0, 8), (1, 64))),
        "down_w": scatter_about(key_of[6], (D, EXPERTS * H), H ** -0.5, 0.1875, ((0, 8), (1, 64))),
    }


def expert_pass(tokens, cotangent, gates_flat, gate_w, up_w, down_w, inputs):
    expert, tok_index, route_index, live = inputs
    live_f = live.astype(jnp.float32)
    rows_in = tokens[tok_index] * live.astype(jnp.bfloat16)[:, None]
    cot_rows = cotangent[tok_index].astype(jnp.float32) * live_f[:, None]
    gate_rows = gates_flat[route_index] * live_f
    w_gate = lax.dynamic_slice_in_dim(gate_w, expert * H, H, 1)
    w_up = lax.dynamic_slice_in_dim(up_w, expert * H, H, 1)
    w_down = lax.dynamic_slice_in_dim(down_w, expert * H, H, 1)
    gate_pre = jnp.dot(rows_in, w_gate, preferred_element_type=jnp.float32)
    up_pre = jnp.dot(rows_in, w_up, preferred_element_type=jnp.float32)
    sigmoid_gate = jax.nn.sigmoid(gate_pre)
    active = gate_pre * sigmoid_gate
    hidden = (active * up_pre).astype(jnp.bfloat16)
    scaled = (gate_rows[:, None] * cot_rows).astype(jnp.bfloat16)
    d_hidden = jnp.dot(scaled, w_down, preferred_element_type=jnp.float32)
    d_gate_pre = (d_hidden * up_pre * sigmoid_gate * (1.0 + gate_pre * (1.0 - sigmoid_gate))).astype(jnp.bfloat16)
    d_up_pre = (d_hidden * active).astype(jnp.bfloat16)
    contract_cols = (((1,), (1,)), ((), ()))
    route_out = jnp.zeros((rows_in.shape[0], D), jnp.float32)
    route_dx = jnp.zeros((rows_in.shape[0], D), jnp.float32)
    for piece in range(SLICES):
        lower = piece * HID_DEV
        upper = lower + HID_DEV
        part_out = lax.dot_general(hidden[:, lower:upper], w_down[:, lower:upper], contract_cols, preferred_element_type=jnp.float32)
        part_out = lax.optimization_barrier(part_out.astype(jnp.bfloat16))
        route_out = route_out + part_out.astype(jnp.float32)
        part_dx = lax.dot_general(d_gate_pre[:, lower:upper], w_gate[:, lower:upper], contract_cols, preferred_element_type=jnp.float32)
        part_dx = part_dx + lax.dot_general(d_up_pre[:, lower:upper], w_up[:, lower:upper], contract_cols, preferred_element_type=jnp.float32)
        part_dx = lax.optimization_barrier(part_dx.astype(jnp.bfloat16))
        route_dx = route_dx + part_dx.astype(jnp.float32)
    weighted_out = gate_rows[:, None] * route_out
    gate_grad = lax.optimization_barrier(jnp.sum(cot_rows * route_out, axis=1))
    per_dp = N_EXPERT * CAP

    def weight_grad(left, right):
        left_f = left.astype(jnp.float32).reshape(N_DP, per_dp, left.shape[1])
        right_f = right.astype(jnp.float32).reshape(N_DP, per_dp, right.shape[1])
        partial_sums = jnp.einsum('nrd,nrh->ndh', left_f, right_f)
        partial_sums = lax.optimization_barrier(partial_sums.astype(jnp.bfloat16))
        return lax.optimization_barrier(jnp.sum(partial_sums.astype(jnp.float32), axis=0)).astype(jnp.bfloat16)
    return (weighted_out, route_dx, gate_grad, weight_grad(rows_in, d_gate_pre), weight_grad(rows_in, d_up_pre), weight_grad(scaled, hidden))

def reference(tokens, cotangent, route_ids, route_gates, gate_w, up_w, down_w):
    blocks = N_DP * N_EXPERT
    routes = TOK_DEV * TOP
    block_ids = route_ids.reshape(blocks, routes)
    matched = (block_ids[:, :, None] == jnp.arange(EXPERTS, dtype=jnp.int32)[None, None, :]).astype(jnp.int32)
    slot_index = jnp.cumsum(matched, axis=1) - 1
    chosen = ((matched[:, :, :, None] == 1) & (slot_index[:, :, :, None] == jnp.arange(CAP, dtype=jnp.int32)[None, None, None, :])).astype(jnp.int32)
    route_pos = lax.optimization_barrier(jnp.sum(chosen * jnp.arange(routes, dtype=jnp.int32)[None, :, None, None], axis=1)).astype(jnp.int32)
    valid = lax.optimization_barrier(jnp.sum(chosen, axis=1)).astype(jnp.int32)
    block_base = jnp.arange(blocks, dtype=jnp.int32)[:, None, None]
    token_index = (block_base * TOK_DEV + route_pos // TOP).astype(jnp.int32)
    flat_route = (block_base * routes + route_pos).astype(jnp.int32)
    token_index = jnp.transpose(token_index, (1, 0, 2)).reshape(EXPERTS, blocks * CAP)
    flat_route = jnp.transpose(flat_route, (1, 0, 2)).reshape(EXPERTS, blocks * CAP)
    valid = jnp.transpose(valid, (1, 0, 2)).reshape(EXPERTS, blocks * CAP)
    gates_flat = route_gates.reshape(TOKENS * TOP)

    def one_expert(inputs):
        return expert_pass(tokens, cotangent, gates_flat, gate_w, up_w, down_w, inputs)
    outs = lax.map(one_expert, (jnp.arange(EXPERTS, dtype=jnp.int32), token_index, flat_route, valid))
    weighted_out, route_dx, gate_grad, grad_gate, grad_up, grad_down = outs
    all_tokens = token_index.reshape(-1)
    moe_out = jnp.zeros((TOKENS, D), jnp.float32).at[all_tokens].add(weighted_out.reshape(-1, D)).astype(jnp.bfloat16)
    d_tokens = jnp.zeros((TOKENS, D), jnp.float32).at[all_tokens].add(route_dx.reshape(-1, D)).astype(jnp.bfloat16)
    d_gates = jnp.zeros((TOKENS * TOP,), jnp.float32).at[flat_route.reshape(-1)].add(gate_grad.reshape(-1)).reshape(TOKENS, TOP)

    def layout(stacked):
        return jnp.transpose(stacked, (1, 0, 2)).reshape(D, EXPERTS * H)
    return (moe_out, d_tokens, d_gates, layout(grad_gate), layout(grad_up), layout(grad_down))
```

```python
import jax
import jax.numpy as jnp
from jax import lax
from jax.sharding import Mesh, PartitionSpec as P

SLICES = 8
CAP = 6
PAD = 8
BF = jnp.bfloat16
F32 = jnp.float32
CONTRACT_COLS = (((1,), (1,)), ((), ()))
CONTRACT_ROWS = (((0,), (0,)), ((), ()))


def dot(a, b, dims=(((1,), (0,)), ((), ()))):
    return lax.dot_general(a, b, dims, preferred_element_type=F32)


def routing(route_ids, route_gates, groups):
    tok_rows = route_ids.shape[0]
    experts = jnp.arange(groups, dtype=jnp.int32)
    match = route_ids[:, :, None] == experts[None, None, :]
    member = jnp.sum(match.astype(F32), axis=1)
    gate = jnp.sum(jnp.where(match, route_gates[:, :, None], 0.0), axis=1)
    row = lax.broadcasted_iota(jnp.int32, (tok_rows, tok_rows), 0)
    col = lax.broadcasted_iota(jnp.int32, (tok_rows, tok_rows), 1)
    before = (col < row).astype(BF)
    slot = dot(before, member.astype(BF))
    return match, member, gate, slot


def shards(tokens, cotangent, route_ids, route_gates, gate_w, up_w, down_w):
    groups = lax.axis_size("y")
    width = tokens.shape[1]
    tok_rows = tokens.shape[0]
    hid = gate_w.shape[1]
    match, member, gate, slot = routing(route_ids, route_gates, groups)
    wide = (jnp.where(member > 0.5, slot, -1.0).T)[:, None, :]
    sel = (wide == jnp.arange(PAD, dtype=F32)[None, :, None]).astype(F32)
    gates_t = gate.T[:, None, :]
    slot_gate = jnp.sum(sel * gates_t, axis=2)
    pick = sel.reshape(groups * PAD, tok_rows).astype(BF)
    token_slots = dot(pick, tokens).astype(BF)
    cot_slots = dot(pick, cotangent)
    scaled_slots = (slot_gate.reshape(groups * PAD, 1) * cot_slots).astype(BF)
    send = jnp.concatenate(
        [token_slots.reshape(groups, PAD, width), scaled_slots.reshape(groups, PAD, width)], axis=1
    )
    w_all = lax.all_gather(
        jnp.concatenate([gate_w, up_w, down_w], axis=1), "dp", axis=0, tiled=True
    )
    w_gate, w_up, w_down = w_all[:, :hid], w_all[:, hid : 2 * hid], w_all[:, 2 * hid :]
    came = lax.all_to_all(send, "y", split_axis=0, concat_axis=0, tiled=True)
    rows = groups * CAP
    out_row = lax.broadcasted_iota(jnp.int32, (2 * rows, groups * 2 * PAD), 0)
    in_row = lax.broadcasted_iota(jnp.int32, (2 * rows, groups * 2 * PAD), 1)
    kind = (out_row >= rows).astype(jnp.int32)
    local = out_row - kind * rows
    wanted = (local // CAP) * (2 * PAD) + kind * PAD + local % CAP
    squeeze = (in_row == wanted).astype(BF)
    compact = dot(squeeze, came.reshape(groups * 2 * PAD, width)).astype(BF)
    both = lax.all_gather(compact, ("x", "c"), axis=0, tiled=False)
    n_slices = both.shape[0]
    token_rows = both[:, :rows].reshape(n_slices * rows, width)
    scaled_rows = both[:, rows:].reshape(n_slices * rows, width)

    gate_pre = dot(token_rows, w_gate)
    up_pre = dot(token_rows, w_up)
    sig = jax.nn.sigmoid(gate_pre)
    active = gate_pre * sig
    hidden = (active * up_pre).astype(BF)
    d_hidden = dot(scaled_rows, w_down)
    d_gate_pre = (d_hidden * up_pre * sig * (1.0 + gate_pre * (1.0 - sig))).astype(BF)
    d_up_pre = (d_hidden * active).astype(BF)
    out_part = dot(hidden, w_down, CONTRACT_COLS).astype(BF)
    dx_part = (
        dot(d_gate_pre, w_gate, CONTRACT_COLS) + dot(d_up_pre, w_up, CONTRACT_COLS)
    ).astype(BF)
    parts = jnp.concatenate(
        [out_part.reshape(n_slices, rows, width), dx_part.reshape(n_slices, rows, width)], axis=1
    ).reshape(n_slices * 2 * rows, width)
    summed = lax.psum_scatter(parts, ("x", "c"), scatter_dimension=0, tiled=True)
    grads = jnp.concatenate(
        [
            dot(token_rows, d_gate_pre, CONTRACT_ROWS),
            dot(token_rows, d_up_pre, CONTRACT_ROWS),
            dot(scaled_rows, hidden, CONTRACT_ROWS),
        ],
        axis=1,
    ).astype(BF)
    grads = lax.psum_scatter(grads, "dp", scatter_dimension=0, tiled=True)
    back = dot(squeeze, summed, CONTRACT_ROWS).astype(BF).reshape(groups, 2 * PAD, width)
    back = lax.all_to_all(back, "y", split_axis=0, concat_axis=0, tiled=True)
    back = back.reshape(groups * 2 * PAD, width)

    zero = jnp.zeros_like(sel)
    member_out = jnp.concatenate([sel, zero], axis=1).reshape(groups * 2 * PAD, tok_rows)
    member_dx = jnp.concatenate([zero, sel], axis=1).reshape(groups * 2 * PAD, tok_rows)
    weight = jnp.concatenate([sel * gates_t, zero], axis=1).reshape(groups * 2 * PAD, tok_rows)
    high = weight.astype(BF)
    low = (weight - high.astype(F32)).astype(BF)
    moe_out = (dot(high, back, CONTRACT_ROWS) + dot(low, back, CONTRACT_ROWS)).astype(BF)
    d_tokens = dot(member_dx.astype(BF), back, CONTRACT_ROWS).astype(BF)
    inner = dot(back, cotangent, CONTRACT_COLS) * member_out
    by_expert = jnp.sum(inner.reshape(groups, 2 * PAD, tok_rows), axis=1).T
    d_gates = jnp.sum(jnp.where(match, by_expert[:, None, :], 0.0), axis=2)
    return (
        moe_out,
        d_tokens,
        d_gates,
        grads[:, :hid],
        grads[:, hid : 2 * hid],
        grads[:, 2 * hid :],
    )


def solution(mesh):
    dp, owners = mesh.devices.shape
    y = owners // SLICES
    grid = Mesh(mesh.devices.reshape(dp, y, SLICES // 2, 2), ("dp", "y", "x", "c"))
    rows = P(("dp", "y", "x", "c"), None)
    cols = P("dp", ("y", "x", "c"))
    return jax.shard_map(
        shards,
        mesh=grid,
        in_specs=(rows, rows, rows, rows, cols, cols, cols),
        out_specs=(rows, rows, rows, cols, cols, cols),
        check_vma=False,
    )
```

```python
import functools

import jax
import jax.numpy as jnp
import numpy as np
from jax import lax
from jax.experimental import pallas as pl
from jax.experimental.pallas import tpu as pltpu
from jax.sharding import Mesh, PartitionSpec as P

SLICES = 8
CAP = 6
PAD = 8
BF = jnp.bfloat16
F32 = jnp.float32
CONTRACT_COLS = (((1,), (1,)), ((), ()))
CONTRACT_ROWS = (((0,), (0,)), ((), ()))


def dot(a, b, dims=(((1,), (0,)), ((), ()))):
    return lax.dot_general(a, b, dims, preferred_element_type=F32)


def squeeze_matrix(groups):
    rows = groups * CAP
    out_row = np.arange(2 * rows)
    kind = out_row // rows
    local = out_row % rows
    wanted = (local // CAP) * (2 * PAD) + kind * PAD + local % CAP
    return jnp.asarray(np.arange(groups * 2 * PAD)[None, :] == wanted[:, None], BF)


def push(src, dst, send, recv, where):
    return pltpu.make_async_remote_copy(
        src_ref=src, dst_ref=dst, send_sem=send, recv_sem=recv,
        device_id=where, device_id_type=pl.DeviceIdType.MESH,
    )


RIGHT, LEFT, PAIR, FAR, PAIR_L, PAIR_R, PAIR_FAR = range(7)


def gather_kernel(nz, ny, nx, chunks, send_ref, w_ref, squeeze_ref, tok_ref, scl_ref, wall_ref,
                  came, y_send, y_recv, x_send, x_recv, z_send, z_recv):
    z, y, x, c = (lax.axis_index(n) for n in ("dp", "y", "x", "c"))
    width = send_ref.shape[2]
    step = width // chunks
    half = w_ref.shape[0] // 2
    x_right, x_left, x_far = (lax.rem(x + k, nx) for k in (1, nx - 1, 2))
    z_right, z_left = lax.rem(z + 1, nz), lax.rem(z + nz - 1, nz)
    mine = x * 2 + c
    outs = (tok_ref, scl_ref)
    rows = tok_ref.shape[1]
    peers = [{"y": lax.rem(y + k, ny)} for k in range(1, ny)]
    peers += [{"x": x_right}, {"x": x_left}, {"c": 1 - c}, {"dp": z_right}, {"dp": z_left}]
    barrier = pltpu.get_barrier_semaphore()
    for peer in peers:
        pl.semaphore_signal(barrier, inc=1, device_id=peer, device_id_type=pl.DeviceIdType.MESH)
    pl.semaphore_wait(barrier, len(peers))

    def z_copy(way, s):
        source = lax.rem(z + (nz - s if way == 0 else s), nz)
        part = pl.ds(0, 2 * half) if s < nz // 2 - 1 else pl.ds(way * half, half)
        src = w_ref if s == 0 else wall_ref.at[source]
        return push(src.at[part, :], wall_ref.at[source, part, :], z_send.at[way, s],
                    z_recv.at[way, s], {"dp": z_right if way == 0 else z_left})

    def y_copy(j, k):
        target = lax.rem(y + k, ny)
        cols = pl.ds(j * step, step)
        return push(send_ref.at[target, :, cols], came.at[y, :, cols], y_send.at[j, k - 1],
                    y_recv.at[j, k - 1], {"y": target})

    def x_copy(kind, j, h):
        cols = pl.ds(j * step, step)
        source = {RIGHT: mine, LEFT: mine, PAIR: mine,
                  FAR: (x_left if h == 0 else x_right) * 2 + c,
                  PAIR_L: x_left * 2 + c, PAIR_R: x_right * 2 + c, PAIR_FAR: x_far * 2 + c}[kind]
        if kind == RIGHT or (kind == FAR and h == 0):
            where = {"x": x_right}
        elif kind == LEFT or kind == FAR:
            where = {"x": x_left}
        else:
            where = {"c": 1 - c}
        ref = outs[h].at[source, :, cols]
        return push(ref, ref, x_send.at[kind, j, h], x_recv.at[kind, j, h], where)

    def both(kind, j):
        return [x_copy(kind, j, h) for h in range(2)]

    started = []

    def start(copies):
        for copy in copies:
            copy.start()
        started.extend(copies)

    def pass_near(j):
        for kind, forward, h in ((RIGHT, PAIR_L, 0), (LEFT, PAIR_R, 1)):
            for copy in both(kind, j):
                copy.wait_recv()
            start([x_copy(FAR, j, h)] + both(forward, j))

    def pass_far(j):
        for h in range(2):
            x_copy(FAR, j, h).wait_recv()
            start([x_copy(PAIR_FAR, j, h)])

    def z_next(s):
        for way in range(2):
            z_copy(way, s - 1).wait_recv()
            start([z_copy(way, s)])

    start([z_copy(0, 0), z_copy(1, 0)])
    for j in range(chunks):
        start([y_copy(j, k) for k in range(1, ny)])
    came[pl.ds(y, 1)] = send_ref[pl.ds(y, 1)]
    wall_ref[pl.ds(z, 1)] = w_ref[...].reshape(1, *w_ref.shape)
    z_steps = list(range(1, nz // 2))
    for j in range(chunks):
        cols = pl.ds(j * step, step)
        for k in range(1, ny):
            y_copy(j, k).wait_recv()
        block = came[:, :, cols].reshape(came.shape[0] * came.shape[1], step)
        packed = dot(squeeze_ref[...], block).astype(BF)
        tok_ref[pl.ds(mine, 1), :, cols] = packed[:rows].reshape(1, rows, step)
        scl_ref[pl.ds(mine, 1), :, cols] = packed[rows:].reshape(1, rows, step)
        start(both(RIGHT, j) + both(LEFT, j) + both(PAIR, j))
        if j >= 1:
            pass_near(j - 1)
            if z_steps:
                z_next(z_steps.pop(0))
        if j >= 2:
            pass_far(j - 2)
    pass_near(chunks - 1)
    for s in z_steps:
        z_next(s)
    for j in range(max(chunks - 2, 0), chunks):
        pass_far(j)
    for way in range(2):
        z_copy(way, nz // 2 - 1).wait_recv()
    for j in range(chunks):
        for kind in (PAIR, PAIR_L, PAIR_R, PAIR_FAR):
            for copy in both(kind, j):
                copy.wait_recv()
    for copy in started:
        copy.wait_send()


def gather(send, weights):
    nz, ny, nx = lax.axis_size("dp"), lax.axis_size("y"), lax.axis_size("x")
    width = send.shape[2]
    chunks = 4
    rows = ny * CAP
    vmem = pl.BlockSpec(memory_space=pltpu.VMEM)
    block = jax.ShapeDtypeStruct((2 * nx, rows, width), BF)
    return pl.pallas_call(
        functools.partial(gather_kernel, nz, ny, nx, chunks),
        out_shape=(block, block, jax.ShapeDtypeStruct((nz, *weights.shape), BF)),
        in_specs=[vmem] * 3,
        out_specs=(vmem,) * 3,
        scratch_shapes=[
            pltpu.VMEM(send.shape, BF),
            pltpu.SemaphoreType.DMA((chunks, ny - 1)),
            pltpu.SemaphoreType.DMA((chunks, ny - 1)),
            pltpu.SemaphoreType.DMA((7, chunks, 2)),
            pltpu.SemaphoreType.DMA((7, chunks, 2)),
            pltpu.SemaphoreType.DMA((2, nz // 2)),
            pltpu.SemaphoreType.DMA((2, nz // 2)),
        ],
        compiler_params=pltpu.CompilerParams(
            collective_id=0, has_side_effects=True, vmem_limit_bytes=32 << 20
        ),
        name="gather_rows",
    )(send, weights, squeeze_matrix(ny))


def routing(route_ids, route_gates, groups):
    tok_rows = route_ids.shape[0]
    experts = jnp.arange(groups, dtype=jnp.int32)
    match = route_ids[:, :, None] == experts[None, None, :]
    member = jnp.sum(match.astype(F32), axis=1)
    gate = jnp.sum(jnp.where(match, route_gates[:, :, None], 0.0), axis=1)
    row = lax.broadcasted_iota(jnp.int32, (tok_rows, tok_rows), 0)
    col = lax.broadcasted_iota(jnp.int32, (tok_rows, tok_rows), 1)
    before = (col < row).astype(BF)
    slot = dot(before, member.astype(BF))
    return match, member, gate, slot


def shards(tokens, cotangent, route_ids, route_gates, gate_w, up_w, down_w):
    groups = lax.axis_size("y")
    width = tokens.shape[1]
    tok_rows = tokens.shape[0]
    hid = gate_w.shape[1]
    match, member, gate, slot = routing(route_ids, route_gates, groups)
    wide = (jnp.where(member > 0.5, slot, -1.0).T)[:, None, :]
    sel = (wide == jnp.arange(PAD, dtype=F32)[None, :, None]).astype(F32)
    gates_t = gate.T[:, None, :]
    slot_gate = jnp.sum(sel * gates_t, axis=2)
    pick = sel.reshape(groups * PAD, tok_rows).astype(BF)
    token_slots = dot(pick, tokens).astype(BF)
    cot_slots = dot(pick, cotangent)
    scaled_slots = (slot_gate.reshape(groups * PAD, 1) * cot_slots).astype(BF)
    send = jnp.concatenate(
        [token_slots.reshape(groups, PAD, width), scaled_slots.reshape(groups, PAD, width)], axis=1
    )
    rows = groups * CAP
    token_rows, scaled_rows, w_all = gather(
        send, jnp.concatenate([gate_w, up_w, down_w], axis=1)
    )
    n_slices = token_rows.shape[0]
    token_rows = token_rows.reshape(n_slices * rows, width)
    scaled_rows = scaled_rows.reshape(n_slices * rows, width)
    w_all = w_all.reshape(width, 3 * hid)
    w_gate, w_up, w_down = w_all[:, :hid], w_all[:, hid : 2 * hid], w_all[:, 2 * hid :]

    gate_pre = dot(token_rows, w_gate)
    up_pre = dot(token_rows, w_up)
    sig = jax.nn.sigmoid(gate_pre)
    active = gate_pre * sig
    hidden = (active * up_pre).astype(BF)
    d_hidden = dot(scaled_rows, w_down)
    d_gate_pre = (d_hidden * up_pre * sig * (1.0 + gate_pre * (1.0 - sig))).astype(BF)
    d_up_pre = (d_hidden * active).astype(BF)
    out_part = dot(hidden, w_down, CONTRACT_COLS).astype(BF)
    dx_part = (
        dot(d_gate_pre, w_gate, CONTRACT_COLS) + dot(d_up_pre, w_up, CONTRACT_COLS)
    ).astype(BF)
    parts = jnp.concatenate(
        [out_part.reshape(n_slices, rows, width), dx_part.reshape(n_slices, rows, width)], axis=1
    ).reshape(n_slices * 2 * rows, width)
    summed = lax.psum_scatter(parts, ("x", "c"), scatter_dimension=0, tiled=True)
    grads = jnp.concatenate(
        [
            dot(token_rows, d_gate_pre, CONTRACT_ROWS),
            dot(token_rows, d_up_pre, CONTRACT_ROWS),
            dot(scaled_rows, hidden, CONTRACT_ROWS),
        ],
        axis=1,
    ).astype(BF)
    grads = lax.psum_scatter(grads, "dp", scatter_dimension=0, tiled=True)
    back = dot(squeeze_matrix(groups), summed, CONTRACT_ROWS).astype(BF).reshape(groups, 2 * PAD, width)
    back = lax.all_to_all(back, "y", split_axis=0, concat_axis=0, tiled=True)
    back = back.reshape(groups * 2 * PAD, width)

    zero = jnp.zeros_like(sel)
    member_out = jnp.concatenate([sel, zero], axis=1).reshape(groups * 2 * PAD, tok_rows)
    member_dx = jnp.concatenate([zero, sel], axis=1).reshape(groups * 2 * PAD, tok_rows)
    weight = jnp.concatenate([sel * gates_t, zero], axis=1).reshape(groups * 2 * PAD, tok_rows)
    high = weight.astype(BF)
    low = (weight - high.astype(F32)).astype(BF)
    moe_out = (dot(high, back, CONTRACT_ROWS) + dot(low, back, CONTRACT_ROWS)).astype(BF)
    d_tokens = dot(member_dx.astype(BF), back, CONTRACT_ROWS).astype(BF)
    inner = dot(back, cotangent, CONTRACT_COLS) * member_out
    by_expert = jnp.sum(inner.reshape(groups, 2 * PAD, tok_rows), axis=1).T
    d_gates = jnp.sum(jnp.where(match, by_expert[:, None, :], 0.0), axis=2)
    return (
        moe_out,
        d_tokens,
        d_gates,
        grads[:, :hid],
        grads[:, hid : 2 * hid],
        grads[:, 2 * hid :],
    )


def solution(mesh):
    dp, owners = mesh.devices.shape
    y = owners // SLICES
    grid = Mesh(mesh.devices.reshape(dp, y, SLICES // 2, 2), ("dp", "y", "x", "c"))
    rows = P(("dp", "y", "x", "c"), None)
    cols = P("dp", ("y", "x", "c"))
    return jax.shard_map(
        shards,
        mesh=grid,
        in_specs=(rows, rows, rows, rows, cols, cols, cols),
        out_specs=(rows, rows, rows, cols, cols, cols),
        check_vma=False,
    )
```

```python
import functools

import jax
import jax.numpy as jnp
import numpy as np
from jax import lax
from jax.experimental import pallas as pl
from jax.experimental.pallas import tpu as pltpu
from jax.sharding import Mesh, PartitionSpec as P

SLICES = 8
CAP = 6
PAD = 8
BF = jnp.bfloat16
F32 = jnp.float32
CONTRACT_COLS = (((1,), (1,)), ((), ()))
CONTRACT_ROWS = (((0,), (0,)), ((), ()))


def dot(a, b, dims=(((1,), (0,)), ((), ()))):
    return lax.dot_general(a, b, dims, preferred_element_type=F32)


def squeeze_matrix(groups):
    rows = groups * CAP
    out_row = np.arange(2 * rows)
    kind = out_row // rows
    local = out_row % rows
    wanted = (local // CAP) * (2 * PAD) + kind * PAD + local % CAP
    return jnp.asarray(np.arange(groups * 2 * PAD)[None, :] == wanted[:, None], BF)


def push(src, dst, send, recv, where):
    return pltpu.make_async_remote_copy(
        src_ref=src, dst_ref=dst, send_sem=send, recv_sem=recv,
        device_id=where, device_id_type=pl.DeviceIdType.MESH,
    )


RIGHT, LEFT, PAIR, FAR, PAIR_L, PAIR_R, PAIR_FAR = range(7)


def gather_kernel(nz, ny, nx, chunks, send_ref, w_ref, squeeze_ref, tok_ref, scl_ref, wall_ref,
                  came, y_send, y_recv, x_send, x_recv, z_send, z_recv):
    z, y, x, c = (lax.axis_index(n) for n in ("dp", "y", "x", "c"))
    width = send_ref.shape[2]
    step = width // chunks
    half = w_ref.shape[0] // 2
    x_right, x_left, x_far = (lax.rem(x + k, nx) for k in (1, nx - 1, 2))
    z_right, z_left = lax.rem(z + 1, nz), lax.rem(z + nz - 1, nz)
    mine = x * 2 + c
    outs = (tok_ref, scl_ref)
    rows = tok_ref.shape[1]
    peers = [{"y": lax.rem(y + k, ny)} for k in range(1, ny)]
    peers += [{"x": x_right}, {"x": x_left}, {"c": 1 - c}, {"dp": z_right}, {"dp": z_left}]
    barrier = pltpu.get_barrier_semaphore()
    for peer in peers:
        pl.semaphore_signal(barrier, inc=1, device_id=peer, device_id_type=pl.DeviceIdType.MESH)
    pl.semaphore_wait(barrier, len(peers))

    def z_copy(way, s):
        source = lax.rem(z + (nz - s if way == 0 else s), nz)
        part = pl.ds(0, 2 * half) if s < nz // 2 - 1 else pl.ds(way * half, half)
        src = w_ref if s == 0 else wall_ref.at[source]
        return push(src.at[part, :], wall_ref.at[source, part, :], z_send.at[way, s],
                    z_recv.at[way, s], {"dp": z_right if way == 0 else z_left})

    def y_copy(j, k):
        target = lax.rem(y + k, ny)
        cols = pl.ds(j * step, step)
        return push(send_ref.at[target, :, cols], came.at[y, :, cols], y_send.at[j, k - 1],
                    y_recv.at[j, k - 1], {"y": target})

    def x_copy(kind, j, h):
        cols = pl.ds(j * step, step)
        source = {RIGHT: mine, LEFT: mine, PAIR: mine,
                  FAR: (x_left if h == 0 else x_right) * 2 + c,
                  PAIR_L: x_left * 2 + c, PAIR_R: x_right * 2 + c, PAIR_FAR: x_far * 2 + c}[kind]
        if kind == RIGHT or (kind == FAR and h == 0):
            where = {"x": x_right}
        elif kind == LEFT or kind == FAR:
            where = {"x": x_left}
        else:
            where = {"c": 1 - c}
        ref = outs[h].at[source, :, cols]
        return push(ref, ref, x_send.at[kind, j, h], x_recv.at[kind, j, h], where)

    def both(kind, j):
        return [x_copy(kind, j, h) for h in range(2)]

    started = []

    def start(copies):
        for copy in copies:
            copy.start()
        started.extend(copies)

    def pass_near(j):
        for kind, forward, h in ((RIGHT, PAIR_L, 0), (LEFT, PAIR_R, 1)):
            for copy in both(kind, j):
                copy.wait_recv()
            start([x_copy(FAR, j, h)] + both(forward, j))

    def pass_far(j):
        for h in range(2):
            x_copy(FAR, j, h).wait_recv()
            start([x_copy(PAIR_FAR, j, h)])

    def z_next(s):
        for way in range(2):
            z_copy(way, s - 1).wait_recv()
            start([z_copy(way, s)])

    start([z_copy(0, 0), z_copy(1, 0)])
    for j in range(chunks):
        start([y_copy(j, k) for k in range(1, ny)])
    came[pl.ds(y, 1)] = send_ref[pl.ds(y, 1)]
    wall_ref[pl.ds(z, 1)] = w_ref[...].reshape(1, *w_ref.shape)
    z_steps = list(range(1, nz // 2))
    for j in range(chunks):
        cols = pl.ds(j * step, step)
        for k in range(1, ny):
            y_copy(j, k).wait_recv()
        block = came[:, :, cols].reshape(came.shape[0] * came.shape[1], step)
        packed = dot(squeeze_ref[...], block).astype(BF)
        tok_ref[pl.ds(mine, 1), :, cols] = packed[:rows].reshape(1, rows, step)
        scl_ref[pl.ds(mine, 1), :, cols] = packed[rows:].reshape(1, rows, step)
        start(both(RIGHT, j) + both(LEFT, j) + both(PAIR, j))
        if j >= 1:
            pass_near(j - 1)
            if z_steps:
                z_next(z_steps.pop(0))
        if j >= 2:
            pass_far(j - 2)
    pass_near(chunks - 1)
    for s in z_steps:
        z_next(s)
    for j in range(max(chunks - 2, 0), chunks):
        pass_far(j)
    for way in range(2):
        z_copy(way, nz // 2 - 1).wait_recv()
    for j in range(chunks):
        for kind in (PAIR, PAIR_L, PAIR_R, PAIR_FAR):
            for copy in both(kind, j):
                copy.wait_recv()
    for copy in started:
        copy.wait_send()


def gather(send, weights):
    nz, ny, nx = lax.axis_size("dp"), lax.axis_size("y"), lax.axis_size("x")
    width = send.shape[2]
    chunks = 4
    rows = ny * CAP
    vmem = pl.BlockSpec(memory_space=pltpu.VMEM)
    block = jax.ShapeDtypeStruct((2 * nx, rows, width), BF)
    return pl.pallas_call(
        functools.partial(gather_kernel, nz, ny, nx, chunks),
        out_shape=(block, block, jax.ShapeDtypeStruct((nz, *weights.shape), BF)),
        in_specs=[vmem] * 3,
        out_specs=(vmem,) * 3,
        scratch_shapes=[
            pltpu.VMEM(send.shape, BF),
            pltpu.SemaphoreType.DMA((chunks, ny - 1)),
            pltpu.SemaphoreType.DMA((chunks, ny - 1)),
            pltpu.SemaphoreType.DMA((7, chunks, 2)),
            pltpu.SemaphoreType.DMA((7, chunks, 2)),
            pltpu.SemaphoreType.DMA((2, nz // 2)),
            pltpu.SemaphoreType.DMA((2, nz // 2)),
        ],
        compiler_params=pltpu.CompilerParams(
            collective_id=0, has_side_effects=True, vmem_limit_bytes=32 << 20
        ),
        name="gather_rows",
    )(send, weights, squeeze_matrix(ny))


def scatter_kernel(nz, ny, nx, chunks, out_ref, dx_ref, g_ref, expand_ref,
                   back_ref, dg_ref, du_ref, dd_ref,
                   pair, far_out, far_in, near_out, near_in, y_out, z_out, z_in,
                   pair_send, pair_recv, far_send, far_recv, near_send, near_recv,
                   y_send, y_recv, z_send, z_recv):
    z, y, x, c = (lax.axis_index(n) for n in ("dp", "y", "x", "c"))
    width = out_ref.shape[3]
    rows = out_ref.shape[2]
    step = width // chunks
    block = g_ref.shape[1]
    half = block // 2
    last = nz // 2 - 1
    x_right, x_left, x_far = (lax.rem(x + k, nx) for k in (1, nx - 1, 2))
    z_right, z_left = lax.rem(z + 1, nz), lax.rem(z + nz - 1, nz)
    parts = (out_ref, dx_ref)
    peers = [{"y": lax.rem(y + k, ny)} for k in range(1, ny)]
    peers += [{"x": x_right}, {"x": x_left}, {"c": 1 - c}, {"dp": z_right}, {"dp": z_left}]
    barrier = pltpu.get_barrier_semaphore()
    for peer in peers:
        pl.semaphore_signal(barrier, inc=1, device_id=peer, device_id_type=pl.DeviceIdType.MESH)
    pl.semaphore_wait(barrier, len(peers))
    sides = ({"x": x_right}, {"x": x_left})
    near = (x_right, x_left)

    def pair_copy(j, h):
        cols = pl.ds(j * step, step)
        return push(parts[h].at[:, 1 - c, :, cols], pair.at[h, :, :, cols], pair_send.at[j, h],
                    pair_recv.at[j, h], {"c": 1 - c})

    def far_copy(j, h):
        cols = pl.ds(j * step, step)
        return push(far_out.at[h, :, cols], far_in.at[h, :, cols], far_send.at[j, h],
                    far_recv.at[j, h], sides[h])

    def near_copy(j, side, h):
        cols = pl.ds(j * step, step)
        return push(near_out.at[side, h, :, cols], near_in.at[side, h, :, cols],
                    near_send.at[j, side, h], near_recv.at[j, side, h], sides[side])

    def y_copy(j, k):
        target = lax.rem(y + k, ny)
        cols = pl.ds(j * step, step)
        return push(y_out.at[target, :, cols], back_ref.at[y, :, cols], y_send.at[j, k - 1],
                    y_recv.at[j, k - 1], {"y": target})

    def z_part(way, s):
        return pl.ds(way * half, half) if s == 0 else pl.ds(0, block)

    def z_dest(way, s):
        return lax.rem(z + (nz // 2 - s if way == 0 else nz // 2 + s), nz)

    def z_copy(way, s):
        part = z_part(way, s)
        src = g_ref.at[z_dest(way, s), part, :] if s == 0 else z_out.at[way, s - 1]
        return push(src, z_in.at[way, s, part, :], z_send.at[way, s], z_recv.at[way, s],
                    {"dp": z_right if way == 0 else z_left})

    started = []

    def start(copy):
        copy.start()
        started.append(copy)

    def z_next(s):
        for way in range(2):
            z_copy(way, s - 1).wait_recv()
            dest = z_dest(way, s)
            for k in range(2):
                rows_k = pl.ds(k * half, half)
                value = g_ref[dest, rows_k, :]
                if s > 1 or k == way:
                    value = (value.astype(F32) + z_in[way, s - 1, rows_k, :].astype(F32)).astype(BF)
                z_out[way, s - 1, rows_k, :] = value
            start(z_copy(way, s))

    def chip_sum(j, h, owner):
        cols = pl.ds(j * step, step)
        return parts[h][owner, c, :, cols].astype(F32) + pair[h, owner, :, cols].astype(F32)

    def first(j):
        cols = pl.ds(j * step, step)
        for h in range(2):
            pair_copy(j, h).wait_recv()
        for h in range(2):
            far_out[h, :, cols] = chip_sum(j, h, x_far).astype(BF)
            start(far_copy(j, h))
        for side in range(2):
            near_out[side, 1 - side, :, cols] = chip_sum(j, 1 - side, near[side]).astype(BF)
            start(near_copy(j, side, 1 - side))

    def middle(j):
        cols = pl.ds(j * step, step)
        for h in range(2):
            far_copy(j, h).wait_recv()
            value = chip_sum(j, h, near[h]) + far_in[h, :, cols].astype(F32)
            near_out[h, h, :, cols] = value.astype(BF)
            start(near_copy(j, h, h))

    def finish(j):
        cols = pl.ds(j * step, step)
        sums = []
        for h in range(2):
            value = chip_sum(j, h, x)
            for side in range(2):
                near_copy(j, side, h).wait_recv()
                value = value + near_in[side, h, :, cols].astype(F32)
            sums.append(value.astype(BF))
        value = dot(expand_ref[...], jnp.concatenate(sums, axis=0)).astype(BF)
        y_out[:, :, cols] = value.reshape(ny, value.shape[0] // ny, step)
        for k in range(1, ny):
            start(y_copy(j, k))
        back_ref[pl.ds(y, 1), :, cols] = y_out[pl.ds(y, 1), :, cols]

    for j in range(chunks):
        for h in range(2):
            start(pair_copy(j, h))
    for way in range(2):
        start(z_copy(way, 0))
    z_steps = list(range(1, last + 1))
    for j in range(chunks):
        first(j)
        if j >= 1:
            middle(j - 1)
        if j >= 2:
            finish(j - 2)
        if j >= 1 and z_steps:
            z_next(z_steps.pop(0))
    middle(chunks - 1)
    for j in range(max(chunks - 2, 0), chunks):
        finish(j)
    for s in z_steps:
        z_next(s)
    for way in range(2):
        z_copy(way, last).wait_recv()
    hid = dg_ref.shape[1]
    for k, ref in enumerate((dg_ref, du_ref, dd_ref)):
        cols = pl.ds(k * hid, hid)
        total = g_ref[z, :, cols].astype(F32)
        for way in range(2):
            total = total + z_in[way, last, :, cols].astype(F32)
        ref[...] = total.astype(BF)
    for j in range(chunks):
        for k in range(1, ny):
            y_copy(j, k).wait_recv()
    for copy in started:
        copy.wait_send()


def scatter(out_part, dx_part, grads):
    nz, ny, nx = lax.axis_size("dp"), lax.axis_size("y"), lax.axis_size("x")
    rows, width = out_part.shape[2:]
    block, cols = grads.shape[1:]
    chunks = 4
    vmem = pl.BlockSpec(memory_space=pltpu.VMEM)
    sems = pltpu.SemaphoreType.DMA
    grad = jax.ShapeDtypeStruct((block, cols // 3), BF)
    return pl.pallas_call(
        functools.partial(scatter_kernel, nz, ny, nx, chunks),
        out_shape=(jax.ShapeDtypeStruct((ny, 2 * PAD, width), BF), grad, grad, grad),
        in_specs=[vmem] * 4,
        out_specs=(vmem,) * 4,
        scratch_shapes=[
            pltpu.VMEM((2, nx, rows, width), BF),
            pltpu.VMEM((2, rows, width), BF),
            pltpu.VMEM((2, rows, width), BF),
            pltpu.VMEM((2, 2, rows, width), BF),
            pltpu.VMEM((2, 2, rows, width), BF),
            pltpu.VMEM((ny, 2 * PAD, width), BF),
            pltpu.VMEM((2, nz // 2 - 1, block, cols), BF),
            pltpu.VMEM((2, nz // 2, block, cols), BF),
            sems((chunks, 2)), sems((chunks, 2)),
            sems((chunks, 2)), sems((chunks, 2)),
            sems((chunks, 2, 2)), sems((chunks, 2, 2)),
            sems((chunks, ny - 1)), sems((chunks, ny - 1)),
            sems((2, nz // 2)), sems((2, nz // 2)),
        ],
        compiler_params=pltpu.CompilerParams(
            collective_id=1, has_side_effects=True, vmem_limit_bytes=48 << 20
        ),
        name="scatter_sums",
    )(out_part, dx_part, grads, squeeze_matrix(ny).T)


def routing(route_ids, route_gates, groups):
    tok_rows = route_ids.shape[0]
    experts = jnp.arange(groups, dtype=jnp.int32)
    match = route_ids[:, :, None] == experts[None, None, :]
    member = jnp.sum(match.astype(F32), axis=1)
    gate = jnp.sum(jnp.where(match, route_gates[:, :, None], 0.0), axis=1)
    row = lax.broadcasted_iota(jnp.int32, (tok_rows, tok_rows), 0)
    col = lax.broadcasted_iota(jnp.int32, (tok_rows, tok_rows), 1)
    before = (col < row).astype(BF)
    slot = dot(before, member.astype(BF))
    return match, member, gate, slot


def shards(tokens, cotangent, route_ids, route_gates, gate_w, up_w, down_w):
    groups = lax.axis_size("y")
    width = tokens.shape[1]
    tok_rows = tokens.shape[0]
    hid = gate_w.shape[1]
    match, member, gate, slot = routing(route_ids, route_gates, groups)
    wide = (jnp.where(member > 0.5, slot, -1.0).T)[:, None, :]
    sel = (wide == jnp.arange(PAD, dtype=F32)[None, :, None]).astype(F32)
    gates_t = gate.T[:, None, :]
    slot_gate = jnp.sum(sel * gates_t, axis=2)
    pick = sel.reshape(groups * PAD, tok_rows).astype(BF)
    token_slots = dot(pick, tokens).astype(BF)
    cot_slots = dot(pick, cotangent)
    scaled_slots = (slot_gate.reshape(groups * PAD, 1) * cot_slots).astype(BF)
    send = jnp.concatenate(
        [token_slots.reshape(groups, PAD, width), scaled_slots.reshape(groups, PAD, width)], axis=1
    )
    rows = groups * CAP
    token_rows, scaled_rows, w_all = gather(
        send, jnp.concatenate([gate_w, up_w, down_w], axis=1)
    )
    n_slices = token_rows.shape[0]
    token_rows = token_rows.reshape(n_slices * rows, width)
    scaled_rows = scaled_rows.reshape(n_slices * rows, width)
    w_all = w_all.reshape(width, 3 * hid)
    w_gate, w_up, w_down = w_all[:, :hid], w_all[:, hid : 2 * hid], w_all[:, 2 * hid :]

    gate_pre = dot(token_rows, w_gate)
    up_pre = dot(token_rows, w_up)
    sig = jax.nn.sigmoid(gate_pre)
    active = gate_pre * sig
    hidden = (active * up_pre).astype(BF)
    d_hidden = dot(scaled_rows, w_down)
    d_gate_pre = (d_hidden * up_pre * sig * (1.0 + gate_pre * (1.0 - sig))).astype(BF)
    d_up_pre = (d_hidden * active).astype(BF)
    out_part = dot(hidden, w_down, CONTRACT_COLS).astype(BF)
    dx_part = (
        dot(d_gate_pre, w_gate, CONTRACT_COLS) + dot(d_up_pre, w_up, CONTRACT_COLS)
    ).astype(BF)
    grads = jnp.concatenate(
        [
            dot(token_rows, d_gate_pre, CONTRACT_ROWS),
            dot(token_rows, d_up_pre, CONTRACT_ROWS),
            dot(scaled_rows, hidden, CONTRACT_ROWS),
        ],
        axis=1,
    ).astype(BF)
    back, d_gate_w, d_up_w, d_down_w = scatter(
        out_part.reshape(n_slices // 2, 2, rows, width),
        dx_part.reshape(n_slices // 2, 2, rows, width),
        grads.reshape(width // gate_w.shape[0], gate_w.shape[0], 3 * hid),
    )
    back = back.reshape(groups * 2 * PAD, width)

    zero = jnp.zeros_like(sel)
    member_out = jnp.concatenate([sel, zero], axis=1).reshape(groups * 2 * PAD, tok_rows)
    member_dx = jnp.concatenate([zero, sel], axis=1).reshape(groups * 2 * PAD, tok_rows)
    weight = jnp.concatenate([sel * gates_t, zero], axis=1).reshape(groups * 2 * PAD, tok_rows)
    high = weight.astype(BF)
    low = (weight - high.astype(F32)).astype(BF)
    moe_out = (dot(high, back, CONTRACT_ROWS) + dot(low, back, CONTRACT_ROWS)).astype(BF)
    d_tokens = dot(member_dx.astype(BF), back, CONTRACT_ROWS).astype(BF)
    inner = dot(back, cotangent, CONTRACT_COLS) * member_out
    by_expert = jnp.sum(inner.reshape(groups, 2 * PAD, tok_rows), axis=1).T
    d_gates = jnp.sum(jnp.where(match, by_expert[:, None, :], 0.0), axis=2)
    return moe_out, d_tokens, d_gates, d_gate_w, d_up_w, d_down_w


def solution(mesh):
    dp, owners = mesh.devices.shape
    y = owners // SLICES
    grid = Mesh(mesh.devices.reshape(dp, y, SLICES // 2, 2), ("dp", "y", "x", "c"))
    rows = P(("dp", "y", "x", "c"), None)
    cols = P("dp", ("y", "x", "c"))
    return jax.shard_map(
        shards,
        mesh=grid,
        in_specs=(rows, rows, rows, rows, cols, cols, cols),
        out_specs=(rows, rows, rows, cols, cols, cols),
        check_vma=False,
    )
```

```python
import functools

import jax
import jax.numpy as jnp
import numpy as np
from jax import lax
from jax.experimental import pallas as pl
from jax.experimental.pallas import tpu as pltpu
from jax.sharding import Mesh, PartitionSpec as P

SLICES = 8
CAP = 6
PAD = 8
BF = jnp.bfloat16
F32 = jnp.float32
CONTRACT_COLS = (((1,), (1,)), ((), ()))
CONTRACT_ROWS = (((0,), (0,)), ((), ()))


def dot(a, b, dims=(((1,), (0,)), ((), ()))):
    return lax.dot_general(a, b, dims, preferred_element_type=F32)


def squeeze_matrix(groups):
    rows = groups * CAP
    out_row = np.arange(2 * rows)
    kind = out_row // rows
    local = out_row % rows
    wanted = (local // CAP) * (2 * PAD) + kind * PAD + local % CAP
    return jnp.asarray(np.arange(groups * 2 * PAD)[None, :] == wanted[:, None], BF)


def push(src, dst, send, recv, where):
    return pltpu.make_async_remote_copy(
        src_ref=src, dst_ref=dst, send_sem=send, recv_sem=recv,
        device_id=where, device_id_type=pl.DeviceIdType.MESH,
    )


RIGHT, LEFT, PAIR, FAR, PAIR_L, PAIR_R, PAIR_FAR = range(7)


def gather_kernel(nz, ny, nx, chunks, send_ref, w_ref, squeeze_ref, tok_ref, scl_ref, wall_ref,
                  came, y_send, y_recv, x_send, x_recv, z_send, z_recv):
    z, y, x, c = (lax.axis_index(n) for n in ("dp", "y", "x", "c"))
    width = send_ref.shape[2]
    step = width // chunks
    half = w_ref.shape[0] // 2
    x_right, x_left, x_far = (lax.rem(x + k, nx) for k in (1, nx - 1, 2))
    z_right, z_left = lax.rem(z + 1, nz), lax.rem(z + nz - 1, nz)
    mine = x * 2 + c
    outs = (tok_ref, scl_ref)
    rows = tok_ref.shape[1]
    peers = [{"y": lax.rem(y + k, ny)} for k in range(1, ny)]
    peers += [{"x": x_right}, {"x": x_left}, {"c": 1 - c}, {"dp": z_right}, {"dp": z_left}]
    barrier = pltpu.get_barrier_semaphore()
    for peer in peers:
        pl.semaphore_signal(barrier, inc=1, device_id=peer, device_id_type=pl.DeviceIdType.MESH)
    pl.semaphore_wait(barrier, len(peers))

    def z_copy(way, s, q):
        source = lax.rem(z + (nz - s if way == 0 else s), nz)
        part = pl.ds(q * half, half)
        src = w_ref if s == 0 else wall_ref.at[source]
        return push(src.at[part, :], wall_ref.at[source, part, :], z_send.at[way, s, q],
                    z_recv.at[way, s, q], {"dp": z_right if way == 0 else z_left})

    def y_copy(j, k):
        target = lax.rem(y + k, ny)
        cols = pl.ds(j * step, step)
        return push(send_ref.at[target, :, cols], came.at[y, :, cols], y_send.at[j, k - 1],
                    y_recv.at[j, k - 1], {"y": target})

    def x_copy(kind, j, h):
        cols = pl.ds(j * step, step)
        source = {RIGHT: mine, LEFT: mine, PAIR: mine,
                  FAR: (x_left if h == 0 else x_right) * 2 + c,
                  PAIR_L: x_left * 2 + c, PAIR_R: x_right * 2 + c, PAIR_FAR: x_far * 2 + c}[kind]
        if kind == RIGHT or (kind == FAR and h == 0):
            where = {"x": x_right}
        elif kind == LEFT or kind == FAR:
            where = {"x": x_left}
        else:
            where = {"c": 1 - c}
        ref = outs[h].at[source, :, cols]
        return push(ref, ref, x_send.at[kind, j, h], x_recv.at[kind, j, h], where)

    def both(kind, j):
        return [x_copy(kind, j, h) for h in range(2)]

    started = []

    def start(copies):
        for copy in copies:
            copy.start()
        started.extend(copies)

    def pass_near(j):
        for kind, forward, h in ((RIGHT, PAIR_L, 0), (LEFT, PAIR_R, 1)):
            for copy in both(kind, j):
                copy.wait_recv()
            start([x_copy(FAR, j, h)] + both(forward, j))

    def pass_far(j):
        for h in range(2):
            x_copy(FAR, j, h).wait_recv()
            start([x_copy(PAIR_FAR, j, h)])

    last = nz // 2 - 1

    def z_next(s, k):
        for way in range(2):
            q = way if k == 0 else 1 - way
            z_copy(way, s - 1, q).wait_recv()
            if s < last or k == 0:
                start([z_copy(way, s, q)])

    start([z_copy(way, 0, way if k == 0 else 1 - way) for k in range(2) for way in range(2)])
    for j in range(chunks):
        start([y_copy(j, k) for k in range(1, ny)])
    came[pl.ds(y, 1)] = send_ref[pl.ds(y, 1)]
    wall_ref[pl.ds(z, 1)] = w_ref[...].reshape(1, *w_ref.shape)
    z_steps = [(s, k) for s in range(1, nz // 2) for k in range(2)]
    for j in range(chunks):
        cols = pl.ds(j * step, step)
        for k in range(1, ny):
            y_copy(j, k).wait_recv()
        block = came[:, :, cols].reshape(came.shape[0] * came.shape[1], step)
        packed = dot(squeeze_ref[...], block).astype(BF)
        tok_ref[pl.ds(mine, 1), :, cols] = packed[:rows].reshape(1, rows, step)
        scl_ref[pl.ds(mine, 1), :, cols] = packed[rows:].reshape(1, rows, step)
        start(both(RIGHT, j) + both(LEFT, j) + both(PAIR, j))
        if j >= 1:
            pass_near(j - 1)
        if j >= 2:
            pass_far(j - 2)
        if j >= 2 and z_steps:
            z_next(*z_steps.pop(0))
    pass_near(chunks - 1)
    for s, k in z_steps:
        z_next(s, k)
    for j in range(max(chunks - 2, 0), chunks):
        pass_far(j)
    for way in range(2):
        z_copy(way, last, way).wait_recv()
    for j in range(chunks):
        for kind in (PAIR, PAIR_L, PAIR_R, PAIR_FAR):
            for copy in both(kind, j):
                copy.wait_recv()
    for copy in started:
        copy.wait_send()


def gather(send, weights):
    nz, ny, nx = lax.axis_size("dp"), lax.axis_size("y"), lax.axis_size("x")
    width = send.shape[2]
    chunks = 7
    rows = ny * CAP
    vmem = pl.BlockSpec(memory_space=pltpu.VMEM)
    block = jax.ShapeDtypeStruct((2 * nx, rows, width), BF)
    return pl.pallas_call(
        functools.partial(gather_kernel, nz, ny, nx, chunks),
        out_shape=(block, block, jax.ShapeDtypeStruct((nz, *weights.shape), BF)),
        in_specs=[vmem] * 3,
        out_specs=(vmem,) * 3,
        scratch_shapes=[
            pltpu.VMEM(send.shape, BF),
            pltpu.SemaphoreType.DMA((chunks, ny - 1)),
            pltpu.SemaphoreType.DMA((chunks, ny - 1)),
            pltpu.SemaphoreType.DMA((7, chunks, 2)),
            pltpu.SemaphoreType.DMA((7, chunks, 2)),
            pltpu.SemaphoreType.DMA((2, nz // 2, 2)),
            pltpu.SemaphoreType.DMA((2, nz // 2, 2)),
        ],
        compiler_params=pltpu.CompilerParams(
            collective_id=0, has_side_effects=True, vmem_limit_bytes=18 << 20
        ),
        name="gather_rows",
    )(send, weights, squeeze_matrix(ny))


def expert_kernel(tok_ref, scl_ref, w_ref, out_ref, dx_ref, g_ref):
    width = tok_ref.shape[1]
    hid = w_ref.shape[1] // 3
    pre = dot(tok_ref[...], w_ref[:, : 2 * hid])
    gate_pre, up_pre = pre[:, :hid], pre[:, hid:]
    sig = jax.nn.sigmoid(gate_pre)
    active = gate_pre * sig
    hidden = (active * up_pre).astype(BF)
    d_hidden = dot(scl_ref[...], w_ref[:, 2 * hid :])
    d_gate_pre = (d_hidden * up_pre * sig * (1.0 + gate_pre * (1.0 - sig))).astype(BF)
    d_up_pre = (d_hidden * active).astype(BF)
    d_pre = jnp.concatenate([d_gate_pre, d_up_pre], axis=1)
    d_pre_t, hidden_t = d_pre.T, hidden.T
    pieces = 7
    step = width // pieces
    for n in range(pieces):
        part = pl.ds(n * step, step)
        g_ref[part, : 2 * hid] = dot(d_pre_t, tok_ref[:, part]).astype(BF).T
        g_ref[part, 2 * hid :] = dot(hidden_t, scl_ref[:, part]).astype(BF).T
        out_ref[:, part] = dot(hidden, w_ref[part, 2 * hid :], CONTRACT_COLS).astype(BF)
        dx_ref[:, part] = dot(d_pre, w_ref[part, : 2 * hid], CONTRACT_COLS).astype(BF)


def expert_math(token_rows, scaled_rows, w_all):
    vmem = pl.BlockSpec(memory_space=pltpu.VMEM)
    rows = jax.ShapeDtypeStruct(token_rows.shape, BF)
    return pl.pallas_call(
        expert_kernel,
        out_shape=(rows, rows, jax.ShapeDtypeStruct(w_all.shape, BF)),
        in_specs=[vmem] * 3,
        out_specs=(vmem,) * 3,
        compiler_params=pltpu.CompilerParams(vmem_limit_bytes=24 << 20),
        name="expert_math",
    )(token_rows, scaled_rows, w_all)


def scatter_kernel(nz, ny, nx, chunks, out_ref, dx_ref, g_ref, expand_ref,
                   back_ref, dg_ref, du_ref, dd_ref,
                   pair, far_out, far_in, near_out, near_in, y_out, z_out, z_in,
                   pair_send, pair_recv, far_send, far_recv, near_send, near_recv,
                   y_send, y_recv, z_send, z_recv):
    z, y, x, c = (lax.axis_index(n) for n in ("dp", "y", "x", "c"))
    width = out_ref.shape[3]
    rows = out_ref.shape[2]
    step = width // chunks
    block = g_ref.shape[1]
    half = block // 2
    last = nz // 2 - 1
    x_right, x_left, x_far = (lax.rem(x + k, nx) for k in (1, nx - 1, 2))
    z_right, z_left = lax.rem(z + 1, nz), lax.rem(z + nz - 1, nz)
    parts = (out_ref, dx_ref)
    peers = [{"y": lax.rem(y + k, ny)} for k in range(1, ny)]
    peers += [{"x": x_right}, {"x": x_left}, {"c": 1 - c}, {"dp": z_right}, {"dp": z_left}]
    barrier = pltpu.get_barrier_semaphore()
    for peer in peers:
        pl.semaphore_signal(barrier, inc=1, device_id=peer, device_id_type=pl.DeviceIdType.MESH)
    pl.semaphore_wait(barrier, len(peers))
    sides = ({"x": x_right}, {"x": x_left})
    near = (x_right, x_left)

    def pair_copy(j, h):
        cols = pl.ds(j * step, step)
        return push(parts[h].at[:, 1 - c, :, cols], pair.at[h, :, :, cols], pair_send.at[j, h],
                    pair_recv.at[j, h], {"c": 1 - c})

    def far_copy(j, h):
        cols = pl.ds(j * step, step)
        return push(far_out.at[h, :, cols], far_in.at[h, :, cols], far_send.at[j, h],
                    far_recv.at[j, h], sides[h])

    def near_copy(j, side, h):
        cols = pl.ds(j * step, step)
        return push(near_out.at[side, h, :, cols], near_in.at[side, h, :, cols],
                    near_send.at[j, side, h], near_recv.at[j, side, h], sides[side])

    def y_copy(j, k):
        target = lax.rem(y + k, ny)
        cols = pl.ds(j * step, step)
        return push(y_out.at[target, :, cols], back_ref.at[y, :, cols], y_send.at[j, k - 1],
                    y_recv.at[j, k - 1], {"y": target})

    def z_dest(way, s):
        return lax.rem(z + (nz // 2 - s if way == 0 else nz // 2 + s), nz)

    def z_copy(way, s, q):
        part = pl.ds(q * half, half)
        src = g_ref.at[z_dest(way, s), part, :] if s == 0 else z_out.at[way, s - 1, part, :]
        return push(src, z_in.at[way, s, part, :], z_send.at[way, s, q], z_recv.at[way, s, q],
                    {"dp": z_right if way == 0 else z_left})

    started = []

    def start(copy):
        copy.start()
        started.append(copy)

    def z_next(s, k):
        for way in range(2):
            q = 1 - way if k == 0 else way
            part = pl.ds(q * half, half)
            value = g_ref[z_dest(way, s), part, :]
            if s > 1 or q == way:
                z_copy(way, s - 1, q).wait_recv()
                value = (value.astype(F32) + z_in[way, s - 1, part, :].astype(F32)).astype(BF)
            z_out[way, s - 1, part, :] = value
            start(z_copy(way, s, q))

    def chip_sum(j, h, owner):
        cols = pl.ds(j * step, step)
        return parts[h][owner, c, :, cols].astype(F32) + pair[h, owner, :, cols].astype(F32)

    def first(j):
        cols = pl.ds(j * step, step)
        for h in range(2):
            pair_copy(j, h).wait_recv()
        for h in range(2):
            far_out[h, :, cols] = chip_sum(j, h, x_far).astype(BF)
            start(far_copy(j, h))
        for side in range(2):
            near_out[side, 1 - side, :, cols] = chip_sum(j, 1 - side, near[side]).astype(BF)
            start(near_copy(j, side, 1 - side))

    def middle(j):
        cols = pl.ds(j * step, step)
        for h in range(2):
            far_copy(j, h).wait_recv()
            value = chip_sum(j, h, near[h]) + far_in[h, :, cols].astype(F32)
            near_out[h, h, :, cols] = value.astype(BF)
            start(near_copy(j, h, h))

    def finish(j):
        cols = pl.ds(j * step, step)
        sums = []
        for h in range(2):
            value = chip_sum(j, h, x)
            for side in range(2):
                near_copy(j, side, h).wait_recv()
                value = value + near_in[side, h, :, cols].astype(F32)
            sums.append(value.astype(BF))
        value = dot(expand_ref[...], jnp.concatenate(sums, axis=0)).astype(BF)
        y_out[:, :, cols] = value.reshape(ny, value.shape[0] // ny, step)
        for k in range(1, ny):
            start(y_copy(j, k))
        back_ref[pl.ds(y, 1), :, cols] = y_out[pl.ds(y, 1), :, cols]

    for j in range(chunks):
        for h in range(2):
            start(pair_copy(j, h))
    for way in range(2):
        start(z_copy(way, 0, way))
    z_steps = [(s, k) for s in range(1, last + 1) for k in range(2)]
    for j in range(chunks):
        first(j)
        if j >= 1:
            middle(j - 1)
        if j >= 2:
            finish(j - 2)
        if z_steps:
            z_next(*z_steps.pop(0))
    middle(chunks - 1)
    for j in range(max(chunks - 2, 0), chunks):
        finish(j)
    for s, k in z_steps:
        z_next(s, k)
    for way in range(2):
        for q in range(2):
            z_copy(way, last, q).wait_recv()
    hid = dg_ref.shape[1]
    for k, ref in enumerate((dg_ref, du_ref, dd_ref)):
        cols = pl.ds(k * hid, hid)
        total = g_ref[z, :, cols].astype(F32)
        for way in range(2):
            total = total + z_in[way, last, :, cols].astype(F32)
        ref[...] = total.astype(BF)
    for j in range(chunks):
        for k in range(1, ny):
            y_copy(j, k).wait_recv()
    for copy in started:
        copy.wait_send()


def scatter(out_part, dx_part, grads):
    nz, ny, nx = lax.axis_size("dp"), lax.axis_size("y"), lax.axis_size("x")
    rows, width = out_part.shape[2:]
    block, cols = grads.shape[1:]
    chunks = 7
    vmem = pl.BlockSpec(memory_space=pltpu.VMEM)
    sems = pltpu.SemaphoreType.DMA
    grad = jax.ShapeDtypeStruct((block, cols // 3), BF)
    return pl.pallas_call(
        functools.partial(scatter_kernel, nz, ny, nx, chunks),
        out_shape=(jax.ShapeDtypeStruct((ny, 2 * PAD, width), BF), grad, grad, grad),
        in_specs=[vmem] * 4,
        out_specs=(vmem,) * 4,
        scratch_shapes=[
            pltpu.VMEM((2, nx, rows, width), BF),
            pltpu.VMEM((2, rows, width), BF),
            pltpu.VMEM((2, rows, width), BF),
            pltpu.VMEM((2, 2, rows, width), BF),
            pltpu.VMEM((2, 2, rows, width), BF),
            pltpu.VMEM((ny, 2 * PAD, width), BF),
            pltpu.VMEM((2, nz // 2 - 1, block, cols), BF),
            pltpu.VMEM((2, nz // 2, block, cols), BF),
            sems((chunks, 2)), sems((chunks, 2)),
            sems((chunks, 2)), sems((chunks, 2)),
            sems((chunks, 2, 2)), sems((chunks, 2, 2)),
            sems((chunks, ny - 1)), sems((chunks, ny - 1)),
            sems((2, nz // 2, 2)), sems((2, nz // 2, 2)),
        ],
        compiler_params=pltpu.CompilerParams(
            collective_id=1, has_side_effects=True, vmem_limit_bytes=26 << 20
        ),
        name="scatter_sums",
    )(out_part, dx_part, grads, squeeze_matrix(ny).T)


def routing(route_ids, route_gates, groups):
    tok_rows = route_ids.shape[0]
    experts = jnp.arange(groups, dtype=jnp.int32)
    match = route_ids[:, :, None] == experts[None, None, :]
    member = jnp.sum(match.astype(F32), axis=1)
    gate = jnp.sum(jnp.where(match, route_gates[:, :, None], 0.0), axis=1)
    row = lax.broadcasted_iota(jnp.int32, (tok_rows, tok_rows), 0)
    col = lax.broadcasted_iota(jnp.int32, (tok_rows, tok_rows), 1)
    before = (col < row).astype(BF)
    slot = dot(before, member.astype(BF))
    return match, member, gate, slot


def shards(tokens, cotangent, route_ids, route_gates, gate_w, up_w, down_w):
    groups = lax.axis_size("y")
    width = tokens.shape[1]
    tok_rows = tokens.shape[0]
    hid = gate_w.shape[1]
    match, member, gate, slot = routing(route_ids, route_gates, groups)
    wide = (jnp.where(member > 0.5, slot, -1.0).T)[:, None, :]
    sel = (wide == jnp.arange(PAD, dtype=F32)[None, :, None]).astype(F32)
    gates_t = gate.T[:, None, :]
    slot_gate = jnp.sum(sel * gates_t, axis=2)
    pick = sel.reshape(groups * PAD, tok_rows).astype(BF)
    token_slots = dot(pick, tokens).astype(BF)
    cot_slots = dot(pick, cotangent)
    scaled_slots = (slot_gate.reshape(groups * PAD, 1) * cot_slots).astype(BF)
    send = jnp.concatenate(
        [token_slots.reshape(groups, PAD, width), scaled_slots.reshape(groups, PAD, width)], axis=1
    )
    rows = groups * CAP
    token_rows, scaled_rows, w_all = gather(
        send, jnp.concatenate([gate_w, up_w, down_w], axis=1)
    )
    n_slices = token_rows.shape[0]
    token_rows = token_rows.reshape(n_slices * rows, width)
    scaled_rows = scaled_rows.reshape(n_slices * rows, width)
    w_all = w_all.reshape(width, 3 * hid)
    out_part, dx_part, grads = expert_math(token_rows, scaled_rows, w_all)
    back, d_gate_w, d_up_w, d_down_w = scatter(
        out_part.reshape(n_slices // 2, 2, rows, width),
        dx_part.reshape(n_slices // 2, 2, rows, width),
        grads.reshape(width // gate_w.shape[0], gate_w.shape[0], 3 * hid),
    )
    back = back.reshape(groups * 2 * PAD, width)

    zero = jnp.zeros_like(sel)
    member_out = jnp.concatenate([sel, zero], axis=1).reshape(groups * 2 * PAD, tok_rows)
    member_dx = jnp.concatenate([zero, sel], axis=1).reshape(groups * 2 * PAD, tok_rows)
    weight = jnp.concatenate([sel * gates_t, zero], axis=1).reshape(groups * 2 * PAD, tok_rows)
    high = weight.astype(BF)
    low = (weight - high.astype(F32)).astype(BF)
    moe_out = (dot(high, back, CONTRACT_ROWS) + dot(low, back, CONTRACT_ROWS)).astype(BF)
    d_tokens = dot(member_dx.astype(BF), back, CONTRACT_ROWS).astype(BF)
    inner = dot(back, cotangent, CONTRACT_COLS) * member_out
    by_expert = jnp.sum(inner.reshape(groups, 2 * PAD, tok_rows), axis=1).T
    d_gates = jnp.sum(jnp.where(match, by_expert[:, None, :], 0.0), axis=2)
    return moe_out, d_tokens, d_gates, d_gate_w, d_up_w, d_down_w


def solution(mesh):
    dp, owners = mesh.devices.shape
    y = owners // SLICES
    grid = Mesh(mesh.devices.reshape(dp, y, SLICES // 2, 2), ("dp", "y", "x", "c"))
    rows = P(("dp", "y", "x", "c"), None)
    cols = P("dp", ("y", "x", "c"))
    return jax.shard_map(
        shards,
        mesh=grid,
        in_specs=(rows, rows, rows, rows, cols, cols, cols),
        out_specs=(rows, rows, rows, cols, cols, cols),
        check_vma=False,
    )
```

```python
import functools

import jax
import jax.numpy as jnp
import numpy as np
from jax import lax
from jax.experimental import pallas as pl
from jax.experimental.pallas import tpu as pltpu
from jax.sharding import Mesh, PartitionSpec as P

SLICES = 8
CAP = 6
PAD = 8
BF = jnp.bfloat16
F32 = jnp.float32
CONTRACT_COLS = (((1,), (1,)), ((), ()))
CONTRACT_ROWS = (((0,), (0,)), ((), ()))


def dot(a, b, dims=(((1,), (0,)), ((), ()))):
    return lax.dot_general(a, b, dims, preferred_element_type=F32)


def squeeze_matrix(groups):
    rows = groups * CAP
    out_row = np.arange(2 * rows)
    kind = out_row // rows
    local = out_row % rows
    wanted = (local // CAP) * (2 * PAD) + kind * PAD + local % CAP
    return jnp.asarray(np.arange(groups * 2 * PAD)[None, :] == wanted[:, None], BF)


def push(src, dst, send, recv, where):
    return pltpu.make_async_remote_copy(
        src_ref=src, dst_ref=dst, send_sem=send, recv_sem=recv,
        device_id=where, device_id_type=pl.DeviceIdType.MESH,
    )


RIGHT, LEFT, PAIR, FAR, PAIR_L, PAIR_R, PAIR_FAR = range(7)


def gather_kernel(nz, ny, nx, chunks, send_ref, w_ref, squeeze_ref, tok_ref, scl_ref, wall_ref,
                  came, y_send, y_recv, x_send, x_recv, z_send, z_recv):
    z, y, x, c = (lax.axis_index(n) for n in ("dp", "y", "x", "c"))
    width = send_ref.shape[2]
    step = width // chunks
    half = w_ref.shape[0] // 2
    x_right, x_left, x_far = (lax.rem(x + k, nx) for k in (1, nx - 1, 2))
    z_right, z_left = lax.rem(z + 1, nz), lax.rem(z + nz - 1, nz)
    mine = x * 2 + c
    outs = (tok_ref, scl_ref)
    rows = tok_ref.shape[1]
    peers = [{"y": lax.rem(y + k, ny)} for k in range(1, ny)]
    peers += [{"x": x_right}, {"x": x_left}, {"c": 1 - c}, {"dp": z_right}, {"dp": z_left}]
    barrier = pltpu.get_barrier_semaphore()
    for peer in peers:
        pl.semaphore_signal(barrier, inc=1, device_id=peer, device_id_type=pl.DeviceIdType.MESH)
    pl.semaphore_wait(barrier, len(peers))

    def z_copy(way, s, q):
        source = lax.rem(z + (nz - s if way == 0 else s), nz)
        part = pl.ds(q * half, half)
        src = w_ref if s == 0 else wall_ref.at[source]
        return push(src.at[part, :], wall_ref.at[source, part, :], z_send.at[way, s, q],
                    z_recv.at[way, s, q], {"dp": z_right if way == 0 else z_left})

    def y_copy(j, k):
        target = lax.rem(y + k, ny)
        cols = pl.ds(j * step, step)
        return push(send_ref.at[target, :, cols], came.at[y, :, cols], y_send.at[j, k - 1],
                    y_recv.at[j, k - 1], {"y": target})

    def x_copy(kind, j, h):
        cols = pl.ds(j * step, step)
        source = {RIGHT: mine, LEFT: mine, PAIR: mine,
                  FAR: (x_left if h == 0 else x_right) * 2 + c,
                  PAIR_L: x_left * 2 + c, PAIR_R: x_right * 2 + c, PAIR_FAR: x_far * 2 + c}[kind]
        if kind == RIGHT or (kind == FAR and h == 0):
            where = {"x": x_right}
        elif kind == LEFT or kind == FAR:
            where = {"x": x_left}
        else:
            where = {"c": 1 - c}
        ref = outs[h].at[source, :, cols]
        return push(ref, ref, x_send.at[kind, j, h], x_recv.at[kind, j, h], where)

    def both(kind, j):
        return [x_copy(kind, j, h) for h in range(2)]

    started = []

    def start(copies):
        for copy in copies:
            copy.start()
        started.extend(copies)

    def pass_near(j):
        for kind, forward, h in ((RIGHT, PAIR_L, 0), (LEFT, PAIR_R, 1)):
            for copy in both(kind, j):
                copy.wait_recv()
            start([x_copy(FAR, j, h)] + both(forward, j))

    def pass_far(j):
        for h in range(2):
            x_copy(FAR, j, h).wait_recv()
            start([x_copy(PAIR_FAR, j, h)])

    last = nz // 2 - 1

    def z_next(s, k):
        for way in range(2):
            q = way if k == 0 else 1 - way
            z_copy(way, s - 1, q).wait_recv()
            if s < last or k == 0:
                start([z_copy(way, s, q)])

    start([z_copy(way, 0, way if k == 0 else 1 - way) for k in range(2) for way in range(2)])
    for j in range(chunks):
        start([y_copy(j, k) for k in range(1, ny)])
    came[pl.ds(y, 1)] = send_ref[pl.ds(y, 1)]
    wall_ref[pl.ds(z, 1)] = w_ref[...].reshape(1, *w_ref.shape)
    z_steps = [(s, k) for s in range(1, nz // 2) for k in range(2)]
    for j in range(chunks):
        cols = pl.ds(j * step, step)
        for k in range(1, ny):
            y_copy(j, k).wait_recv()
        block = came[:, :, cols].reshape(came.shape[0] * came.shape[1], step)
        packed = dot(squeeze_ref[...], block).astype(BF)
        tok_ref[pl.ds(mine, 1), :, cols] = packed[:rows].reshape(1, rows, step)
        scl_ref[pl.ds(mine, 1), :, cols] = packed[rows:].reshape(1, rows, step)
        start(both(RIGHT, j) + both(LEFT, j) + both(PAIR, j))
        if j >= 1:
            pass_near(j - 1)
        if j >= 2:
            pass_far(j - 2)
        if j >= 1 and z_steps:
            z_next(*z_steps.pop(0))
    pass_near(chunks - 1)
    for s, k in z_steps:
        z_next(s, k)
    for j in range(max(chunks - 2, 0), chunks):
        pass_far(j)
    for way in range(2):
        z_copy(way, last, way).wait_recv()
    for j in range(chunks):
        for kind in (PAIR, PAIR_L, PAIR_R, PAIR_FAR):
            for copy in both(kind, j):
                copy.wait_recv()
    for copy in started:
        copy.wait_send()


def gather(send, weights):
    nz, ny, nx = lax.axis_size("dp"), lax.axis_size("y"), lax.axis_size("x")
    width = send.shape[2]
    chunks = 7
    rows = ny * CAP
    vmem = pl.BlockSpec(memory_space=pltpu.VMEM)
    block = jax.ShapeDtypeStruct((2 * nx, rows, width), BF)
    return pl.pallas_call(
        functools.partial(gather_kernel, nz, ny, nx, chunks),
        out_shape=(block, block, jax.ShapeDtypeStruct((nz, *weights.shape), BF)),
        in_specs=[vmem] * 3,
        out_specs=(vmem,) * 3,
        scratch_shapes=[
            pltpu.VMEM(send.shape, BF),
            pltpu.SemaphoreType.DMA((chunks, ny - 1)),
            pltpu.SemaphoreType.DMA((chunks, ny - 1)),
            pltpu.SemaphoreType.DMA((7, chunks, 2)),
            pltpu.SemaphoreType.DMA((7, chunks, 2)),
            pltpu.SemaphoreType.DMA((2, nz // 2, 2)),
            pltpu.SemaphoreType.DMA((2, nz // 2, 2)),
        ],
        compiler_params=pltpu.CompilerParams(
            collective_id=0, has_side_effects=True, vmem_limit_bytes=18 << 20
        ),
        name="gather_rows",
    )(send, weights, squeeze_matrix(ny))


def expert_kernel(tok_ref, scl_ref, w_ref, out_ref, dx_ref, g_ref):
    width = tok_ref.shape[1]
    hid = w_ref.shape[1] // 3
    pre = dot(tok_ref[...], w_ref[:, : 2 * hid])
    gate_pre, up_pre = pre[:, :hid], pre[:, hid:]
    sig = jax.nn.sigmoid(gate_pre)
    active = gate_pre * sig
    hidden = (active * up_pre).astype(BF)
    d_hidden = dot(scl_ref[...], w_ref[:, 2 * hid :])
    d_gate_pre = (d_hidden * up_pre * sig * (1.0 + gate_pre * (1.0 - sig))).astype(BF)
    d_up_pre = (d_hidden * active).astype(BF)
    d_pre = jnp.concatenate([d_gate_pre, d_up_pre], axis=1)
    d_pre_t, hidden_t = d_pre.T, hidden.T
    pieces = 7
    step = width // pieces
    for n in range(pieces):
        part = pl.ds(n * step, step)
        g_ref[part, : 2 * hid] = dot(d_pre_t, tok_ref[:, part]).astype(BF).T
        g_ref[part, 2 * hid :] = dot(hidden_t, scl_ref[:, part]).astype(BF).T
        out_ref[:, part] = dot(hidden, w_ref[part, 2 * hid :], CONTRACT_COLS).astype(BF)
        dx_ref[:, part] = dot(d_pre, w_ref[part, : 2 * hid], CONTRACT_COLS).astype(BF)


def expert_math(token_rows, scaled_rows, w_all):
    vmem = pl.BlockSpec(memory_space=pltpu.VMEM)
    rows = jax.ShapeDtypeStruct(token_rows.shape, BF)
    return pl.pallas_call(
        expert_kernel,
        out_shape=(rows, rows, jax.ShapeDtypeStruct(w_all.shape, BF)),
        in_specs=[vmem] * 3,
        out_specs=(vmem,) * 3,
        compiler_params=pltpu.CompilerParams(vmem_limit_bytes=24 << 20),
        name="expert_math",
    )(token_rows, scaled_rows, w_all)


def scatter_kernel(nz, ny, nx, chunks, out_ref, dx_ref, g_ref, expand_ref,
                   back_ref, sum_ref,
                   pair, far_out, far_in, near_out, near_in, y_out, z_out, z_in,
                   pair_send, pair_recv, far_send, far_recv, near_send, near_recv,
                   y_send, y_recv, z_send, z_recv):
    z, y, x, c = (lax.axis_index(n) for n in ("dp", "y", "x", "c"))
    width = out_ref.shape[3]
    rows = out_ref.shape[2]
    step = width // chunks
    block = g_ref.shape[1]
    half = block // 2
    last = nz // 2 - 1
    x_right, x_left, x_far = (lax.rem(x + k, nx) for k in (1, nx - 1, 2))
    z_right, z_left = lax.rem(z + 1, nz), lax.rem(z + nz - 1, nz)
    parts = (out_ref, dx_ref)
    peers = [{"y": lax.rem(y + k, ny)} for k in range(1, ny)]
    peers += [{"x": x_right}, {"x": x_left}, {"c": 1 - c}, {"dp": z_right}, {"dp": z_left}]
    barrier = pltpu.get_barrier_semaphore()
    for peer in peers:
        pl.semaphore_signal(barrier, inc=1, device_id=peer, device_id_type=pl.DeviceIdType.MESH)
    pl.semaphore_wait(barrier, len(peers))
    sides = ({"x": x_right}, {"x": x_left})
    near = (x_right, x_left)

    def pair_copy(j, h):
        cols = pl.ds(j * step, step)
        return push(parts[h].at[:, 1 - c, :, cols], pair.at[h, :, :, cols], pair_send.at[j, h],
                    pair_recv.at[j, h], {"c": 1 - c})

    def far_copy(j, h):
        cols = pl.ds(j * step, step)
        return push(far_out.at[h, :, cols], far_in.at[h, :, cols], far_send.at[j, h],
                    far_recv.at[j, h], sides[h])

    def near_copy(j, side, h):
        cols = pl.ds(j * step, step)
        return push(near_out.at[side, h, :, cols], near_in.at[side, h, :, cols],
                    near_send.at[j, side, h], near_recv.at[j, side, h], sides[side])

    def y_copy(j, k):
        target = lax.rem(y + k, ny)
        cols = pl.ds(j * step, step)
        return push(y_out.at[target, :, cols], back_ref.at[y, :, cols], y_send.at[j, k - 1],
                    y_recv.at[j, k - 1], {"y": target})

    def z_dest(way, s):
        return lax.rem(z + (nz // 2 - s if way == 0 else nz // 2 + s), nz)

    def z_copy(way, s, q):
        part = pl.ds(q * half, half)
        src = g_ref.at[z_dest(way, s), part, :] if s == 0 else z_out.at[way, s - 1, part, :]
        return push(src, z_in.at[way, s, part, :], z_send.at[way, s, q], z_recv.at[way, s, q],
                    {"dp": z_right if way == 0 else z_left})

    started = []

    def start(copy):
        copy.start()
        started.append(copy)

    def z_next(s, k):
        for way in range(2):
            q = 1 - way if k == 0 else way
            part = pl.ds(q * half, half)
            value = g_ref[z_dest(way, s), part, :]
            if s > 1 or q == way:
                z_copy(way, s - 1, q).wait_recv()
                value = (value.astype(F32) + z_in[way, s - 1, part, :].astype(F32)).astype(BF)
            z_out[way, s - 1, part, :] = value
            start(z_copy(way, s, q))

    def chip_sum(j, h, owner):
        cols = pl.ds(j * step, step)
        return parts[h][owner, c, :, cols].astype(F32) + pair[h, owner, :, cols].astype(F32)

    def first(j):
        cols = pl.ds(j * step, step)
        for h in range(2):
            pair_copy(j, h).wait_recv()
        for h in range(2):
            far_out[h, :, cols] = chip_sum(j, h, x_far).astype(BF)
            start(far_copy(j, h))
        for side in range(2):
            near_out[side, 1 - side, :, cols] = chip_sum(j, 1 - side, near[side]).astype(BF)
            start(near_copy(j, side, 1 - side))

    def middle(j):
        cols = pl.ds(j * step, step)
        for h in range(2):
            far_copy(j, h).wait_recv()
            value = chip_sum(j, h, near[h]) + far_in[h, :, cols].astype(F32)
            near_out[h, h, :, cols] = value.astype(BF)
            start(near_copy(j, h, h))

    def finish(j):
        cols = pl.ds(j * step, step)
        sums = []
        for h in range(2):
            value = chip_sum(j, h, x)
            for side in range(2):
                near_copy(j, side, h).wait_recv()
                value = value + near_in[side, h, :, cols].astype(F32)
            sums.append(value.astype(BF))
        value = dot(expand_ref[...], jnp.concatenate(sums, axis=0)).astype(BF)
        y_out[:, :, cols] = value.reshape(ny, value.shape[0] // ny, step)
        for k in range(1, ny):
            start(y_copy(j, k))
        back_ref[pl.ds(y, 1), :, cols] = y_out[pl.ds(y, 1), :, cols]

    for j in range(chunks):
        for h in range(2):
            start(pair_copy(j, h))
    for way in range(2):
        start(z_copy(way, 0, way))
    z_steps = [(s, k) for s in range(1, last + 1) for k in range(2)]
    for j in range(chunks):
        first(j)
        if j >= 1:
            middle(j - 1)
        if j >= 2:
            finish(j - 2)
        if z_steps:
            z_next(*z_steps.pop(0))
    middle(chunks - 1)
    for j in range(max(chunks - 2, 0), chunks):
        finish(j)
    for s, k in z_steps:
        z_next(s, k)
    for way in range(2):
        for q in range(2):
            z_copy(way, last, q).wait_recv()
    total = g_ref[z].astype(F32)
    for way in range(2):
        total = total + z_in[way, last].astype(F32)
    sum_ref[...] = total.astype(BF)
    for j in range(chunks):
        for k in range(1, ny):
            y_copy(j, k).wait_recv()
    for copy in started:
        copy.wait_send()


def scatter(out_part, dx_part, grads):
    nz, ny, nx = lax.axis_size("dp"), lax.axis_size("y"), lax.axis_size("x")
    rows, width = out_part.shape[2:]
    block, cols = grads.shape[1:]
    chunks = 7
    vmem = pl.BlockSpec(memory_space=pltpu.VMEM)
    sems = pltpu.SemaphoreType.DMA
    grad = jax.ShapeDtypeStruct((block, cols), BF)
    return pl.pallas_call(
        functools.partial(scatter_kernel, nz, ny, nx, chunks),
        out_shape=(jax.ShapeDtypeStruct((ny, 2 * PAD, width), BF), grad),
        in_specs=[vmem] * 4,
        out_specs=(vmem,) * 2,
        scratch_shapes=[
            pltpu.VMEM((2, nx, rows, width), BF),
            pltpu.VMEM((2, rows, width), BF),
            pltpu.VMEM((2, rows, width), BF),
            pltpu.VMEM((2, 2, rows, width), BF),
            pltpu.VMEM((2, 2, rows, width), BF),
            pltpu.VMEM((ny, 2 * PAD, width), BF),
            pltpu.VMEM((2, nz // 2 - 1, block, cols), BF),
            pltpu.VMEM((2, nz // 2, block, cols), BF),
            sems((chunks, 2)), sems((chunks, 2)),
            sems((chunks, 2)), sems((chunks, 2)),
            sems((chunks, 2, 2)), sems((chunks, 2, 2)),
            sems((chunks, ny - 1)), sems((chunks, ny - 1)),
            sems((2, nz // 2, 2)), sems((2, nz // 2, 2)),
        ],
        compiler_params=pltpu.CompilerParams(
            collective_id=1, has_side_effects=True, vmem_limit_bytes=26 << 20
        ),
        name="scatter_sums",
    )(out_part, dx_part, grads, squeeze_matrix(ny).T)


def routing(route_ids, route_gates, groups):
    tok_rows = route_ids.shape[0]
    experts = jnp.arange(groups, dtype=jnp.int32)
    match = route_ids[:, :, None] == experts[None, None, :]
    member = jnp.sum(match.astype(F32), axis=1)
    gate = jnp.sum(jnp.where(match, route_gates[:, :, None], 0.0), axis=1)
    row = lax.broadcasted_iota(jnp.int32, (tok_rows, tok_rows), 0)
    col = lax.broadcasted_iota(jnp.int32, (tok_rows, tok_rows), 1)
    before = (col < row).astype(BF)
    slot = dot(before, member.astype(BF))
    return match, member, gate, slot


def shards(tokens, cotangent, route_ids, route_gates, gate_w, up_w, down_w):
    groups = lax.axis_size("y")
    width = tokens.shape[1]
    tok_rows = tokens.shape[0]
    hid = gate_w.shape[1]
    match, member, gate, slot = routing(route_ids, route_gates, groups)
    wide = (jnp.where(member > 0.5, slot, -1.0).T)[:, None, :]
    sel = (wide == jnp.arange(PAD, dtype=F32)[None, :, None]).astype(F32)
    gates_t = gate.T[:, None, :]
    slot_gate = jnp.sum(sel * gates_t, axis=2)
    pick = sel.reshape(groups * PAD, tok_rows).astype(BF)
    token_slots = dot(pick, tokens).astype(BF)
    cot_slots = dot(pick, cotangent)
    scaled_slots = (slot_gate.reshape(groups * PAD, 1) * cot_slots).astype(BF)
    send = jnp.concatenate(
        [token_slots.reshape(groups, PAD, width), scaled_slots.reshape(groups, PAD, width)], axis=1
    )
    rows = groups * CAP
    token_rows, scaled_rows, w_all = gather(
        send, jnp.concatenate([gate_w, up_w, down_w], axis=1)
    )
    n_slices = token_rows.shape[0]
    token_rows = token_rows.reshape(n_slices * rows, width)
    scaled_rows = scaled_rows.reshape(n_slices * rows, width)
    w_all = w_all.reshape(width, 3 * hid)
    out_part, dx_part, grads = expert_math(token_rows, scaled_rows, w_all)
    back, summed = scatter(
        out_part.reshape(n_slices // 2, 2, rows, width),
        dx_part.reshape(n_slices // 2, 2, rows, width),
        grads.reshape(width // gate_w.shape[0], gate_w.shape[0], 3 * hid),
    )
    back = back.reshape(groups * 2 * PAD, width)

    zero = jnp.zeros_like(sel)
    member_out = jnp.concatenate([sel, zero], axis=1).reshape(groups * 2 * PAD, tok_rows)
    member_dx = jnp.concatenate([zero, sel], axis=1).reshape(groups * 2 * PAD, tok_rows)
    weight = jnp.concatenate([sel * gates_t, zero], axis=1).reshape(groups * 2 * PAD, tok_rows)
    high = weight.astype(BF)
    low = (weight - high.astype(F32)).astype(BF)
    moe_out = (dot(high, back, CONTRACT_ROWS) + dot(low, back, CONTRACT_ROWS)).astype(BF)
    d_tokens = dot(member_dx.astype(BF), back, CONTRACT_ROWS).astype(BF)
    inner = dot(back, cotangent, CONTRACT_COLS) * member_out
    by_expert = jnp.sum(inner.reshape(groups, 2 * PAD, tok_rows), axis=1).T
    d_gates = jnp.sum(jnp.where(match, by_expert[:, None, :], 0.0), axis=2)
    d_gate_w, d_up_w, d_down_w = jnp.split(summed, 3, axis=1)
    return moe_out, d_tokens, d_gates, d_gate_w, d_up_w, d_down_w


def solution(mesh):
    dp, owners = mesh.devices.shape
    y = owners // SLICES
    grid = Mesh(mesh.devices.reshape(dp, y, SLICES // 2, 2), ("dp", "y", "x", "c"))
    rows = P(("dp", "y", "x", "c"), None)
    cols = P("dp", ("y", "x", "c"))
    return jax.shard_map(
        shards,
        mesh=grid,
        in_specs=(rows, rows, rows, rows, cols, cols, cols),
        out_specs=(rows, rows, rows, cols, cols, cols),
        check_vma=False,
    )
```
